32 devices in a mesh: tm: 16 (over z, x, core), fsdp: 2 (over y).
Axes of the slice: x: 2, y: 2, z: 4, core: 2. Of those that a mesh axis runs over, the one named last changes fastest.
Arguments:
- queries: bfloat16 [16, 256, 3072], P('tm', 'fsdp'), may hold values from -12 to 12
- keys: bfloat16 [16, 256, 3072], P('tm', 'fsdp'), may hold values from -12 to 12
- values: bfloat16 [16, 256, 3072], P('tm', 'fsdp'), may hold values from -6 to 6
Outputs:
- attended: bfloat16 [16, 256, 3072], P('tm', 'fsdp')
The draws below stay inside these ranges and needn't reach their ends.
All inputs are finite; a program needn't handle non-finite values.
Results may differ from the reference program's by a relative error of at most 0.0029.
Values may be sent and summed in bfloat16 or wider, within the bound.
No kernel may reach another device: no remote copies, remote signals or barrier semaphores. Data moves between devices by JAX's collectives and lax.ppermute only.
A program may use at most 64 MiB of HBM per device.

```python
import math
import jax
import jax.numpy as jnp
from jax import lax

H = 24
HD = 128
F = 256
FRAMES = 16


def rough_field(key, salt):
    inner = jax.random.fold_in(key, salt)
    base_values = jnp.clip(jax.random.normal(jax.random.fold_in(inner, 1), (FRAMES, F, H * HD), jnp.float32), -6.0, 6.0)
    row_scale = jnp.exp(jax.random.uniform(jax.random.fold_in(inner, 2), (FRAMES, F, 1), jnp.float32, -0.7, 0.7))
    return base_values * row_scale


def draw_queries(key, part):
    field = rough_field(key, 1)
    return field.astype(jnp.bfloat16)


def draw_keys(key, part):
    field = rough_field(key, 2)
    return field.astype(jnp.bfloat16)


def block_scale(stream_key, shape, cuts, low, largest):
    gain, own = 1.0, jax.random.fold_in(stream_key, 6)
    for position, blocks in cuts:
        draws = jnp.exp(jax.random.uniform(jax.random.fold_in(own, position), (blocks,), jnp.float32, low / len(cuts), largest / len(cuts)))
        gain = gain * jnp.repeat(draws, shape[position] // blocks).reshape([-1 if axis == position else 1 for axis in range(len(shape))])
    return gain


def normal_values(key, shape, width, bound, shards=(), kind=jnp.bfloat16):
    result = width * jax.random.normal(key, shape, jnp.float32)
    if shards:
        result = result * block_scale(key, shape, shards, -0.22, 0.18)
    return jnp.clip(result, -bound, bound).astype(kind)


def setup_inputs(seed: int = 0) -> dict:
    splits = jax.random.split(jax.random.key(seed), 4)
    return {
        "queries": draw_queries(jax.random.fold_in(splits[3], 71), 0),
        "keys": draw_keys(jax.random.fold_in(splits[3], 71), 0),
        "values": normal_values(splits[2], (FRAMES, F, H * HD), 1.0, 6.0, ((0, 16), (1, 2))),
    }


def reference(queries, keys, values):
    scaling = 1.0 / math.sqrt(HD)
    blank_frames = jnp.zeros((2, F, H * HD), keys.dtype)
    padded_keys = jnp.concatenate([blank_frames, keys], axis=0)
    padded_values = jnp.concatenate([blank_frames, values], axis=0)
    key_frame = jnp.arange(3 * F, dtype=jnp.int32) // F

    def one_frame(frame_at):
        window_keys = lax.dynamic_slice_in_dim(padded_keys, frame_at, 3, 0).reshape(3 * F, H, HD).astype(jnp.float32)
        window_values = lax.dynamic_slice_in_dim(padded_values, frame_at, 3, 0).reshape(3 * F, H, HD).astype(jnp.float32)
        queries_now = lax.dynamic_index_in_dim(queries, frame_at, 0, keepdims=False).reshape(F, H, HD).astype(jnp.float32)
        scores = jnp.einsum('fhd,khd->hfk', queries_now, window_keys) * scaling
        usable = frame_at - 2 + key_frame >= 0
        scores = jnp.where(usable[None, None, :], scores, -1e+30)
        peaks = lax.optimization_barrier(jnp.max(scores, axis=-1, keepdims=True))
        weights = jnp.exp(scores - peaks)
        totals = lax.optimization_barrier(jnp.sum(weights, axis=-1, keepdims=True))
        rounded = lax.optimization_barrier(weights.astype(jnp.bfloat16)).astype(jnp.float32)
        mixed = jnp.einsum('hfk,khd->fhd', rounded, window_values) / jnp.transpose(totals, (1, 0, 2))
        return mixed.reshape(F, H * HD).astype(jnp.bfloat16)
    return lax.map(one_frame, jnp.arange(FRAMES, dtype=jnp.int32))
```

```python
import math
import functools

import jax
import jax.numpy as jnp
from jax import lax
from jax.experimental import pallas as pl
from jax.experimental.pallas import tpu as pltpu
from jax.sharding import PartitionSpec as P

HD = 128
GROUPS = 3
SCALE = math.log2(math.e) / math.sqrt(HD)
FAR = 1e30


def rotated(block, axis, distance):
    size = lax.axis_size(axis)
    return lax.ppermute(block, axis, [(i, (i + distance) % size) for i in range(size)])


def shifted(block, axis, distance):
    size = lax.axis_size(axis)
    return lax.ppermute(block, axis, [(i, i + distance) for i in range(size - distance)])


def swapped(block, axis):
    size = lax.axis_size(axis)
    return lax.ppermute(block, axis, [(i, i ^ 1) for i in range(size)])


def attend_kernel(count, *refs):
    q_refs, now, back2, mate_now, mate_back2 = (refs[i * count : (i + 1) * count] for i in range(5))
    outs = refs[5 * count :]
    frame = lax.axis_index("tm")
    odd = (frame % 2) == 1
    rows = q_refs[0].shape[0]

    def scores(q, keys):
        return lax.dot_general(q, keys, (((1,), (1,)), ((), ())), preferred_element_type=jnp.float32)

    for head in range(q_refs[0].shape[1] // HD):
        cols = slice(head * HD, (head + 1) * HD)

        def pick(refs, which):
            return jnp.concatenate([r[which, :, cols] for r in refs], axis=0)

        def pick_mate(which):
            return jnp.concatenate(
                [jnp.where(odd, a[which, :, cols], b[which, :, cols]) for a, b in zip(mate_now, mate_back2)], axis=0
            )

        k0, k1, k2 = pick(now, 0), pick_mate(0), pick(back2, 0)
        v0, v1, v2 = pick(now, 1), pick_mate(1), pick(back2, 1)
        for at in range(0, count, 2):
            some = q_refs[at : at + 2]
            q = jnp.concatenate([r[:, cols] for r in some], axis=0)
            s0, s1, s2 = scores(q, k0), scores(q, k1), scores(q, k2)
            m0, m1, m2 = (jnp.max(s, axis=1, keepdims=True) for s in (s0, s1, s2))
            peak = jnp.maximum(m0, jnp.maximum(jnp.where(frame >= 1, m1, -FAR), jnp.where(frame >= 2, m2, -FAR)))
            peak1 = jnp.where(frame >= 1, peak, FAR)
            peak2 = jnp.where(frame >= 2, peak, FAR)
            p0 = jnp.exp2((s0 - peak) * SCALE)
            p1 = jnp.exp2((s1 - peak1) * SCALE)
            p2 = jnp.exp2((s2 - peak2) * SCALE)
            total = jnp.sum(p0 + p1 + p2, axis=1, keepdims=True)
            mixed = (
                jnp.dot(p0.astype(jnp.bfloat16), v0, preferred_element_type=jnp.float32)
                + jnp.dot(p1.astype(jnp.bfloat16), v1, preferred_element_type=jnp.float32)
                + jnp.dot(p2.astype(jnp.bfloat16), v2, preferred_element_type=jnp.float32)
            )
            mixed = (mixed * (1.0 / total)).astype(jnp.bfloat16)
            for i in range(len(some)):
                outs[at + i][:, cols] = mixed[i * rows : (i + 1) * rows]


def attend(queries, now, back2, mate_now, mate_back2):
    count = len(queries)
    rows, width = queries[0].shape
    heads = width // HD
    work = heads * (count * rows) * (3 * count * rows)
    return pl.pallas_call(
        functools.partial(attend_kernel, count),
        out_shape=[jax.ShapeDtypeStruct((rows, width), jnp.bfloat16)] * count,
        in_specs=[pl.BlockSpec(memory_space=pltpu.VMEM)] * (5 * count),
        out_specs=[pl.BlockSpec(memory_space=pltpu.VMEM)] * count,
        cost_estimate=pl.CostEstimate(
            flops=4 * work * HD, transcendentals=work, bytes_accessed=2 * rows * width * count * 10
        ),
        compiler_params=pltpu.CompilerParams(vmem_limit_bytes=40 * 1024 * 1024),
        name="attend",
    )(*queries, *now, *back2, *mate_now, *mate_back2)


def body(queries, keys, values):
    size = lax.axis_size("fsdp")
    me = lax.axis_index("fsdp")
    q, k, v = queries[0], keys[0], values[0]
    width = q.shape[1] // size
    heads = width // HD
    groups = math.gcd(GROUPS, heads)
    span = width // groups

    def part(x, owner, group):
        return lax.dynamic_slice_in_dim(x, owner * width + group * span, span, 1)

    def pair(owner, group):
        return jnp.stack([part(k, owner, group), part(v, owner, group)])

    outs = []
    for g in range(groups):
        here = [pair(me, g)]
        asked = [part(q, me, g)]
        for r in range(1, size):
            peer = (me + r) % size
            here.append(rotated(pair(peer, g), "fsdp", r))
            asked.append(rotated(part(q, peer, g), "fsdp", r))
        back2 = [shifted(x, "tm", 2) for x in here]
        mate_now = [swapped(x, "tm") for x in here]
        mate_back2 = [swapped(x, "tm") for x in back2]
        outs.append(attend(asked, here, back2, mate_now, mate_back2))
    returned = []
    for r in range(size):
        pieces = [outs[g][r] if r == 0 else rotated(outs[g][r], "fsdp", -r) for g in range(groups)]
        returned.append(jnp.concatenate(pieces, axis=1))
    result = jnp.zeros_like(q)
    for r in range(size):
        result = lax.dynamic_update_slice_in_dim(result, returned[r], ((me + r) % size) * width, 1)
    return result[None]


def solution(mesh):
    spec = P("tm", "fsdp", None)
    return jax.shard_map(body, mesh=mesh, in_specs=(spec, spec, spec), out_specs=spec, check_vma=False)
```

```python
import functools
import math

import jax
import jax.numpy as jnp
from jax import lax
from jax.experimental import pallas as pl
from jax.experimental.pallas import tpu as pltpu
from jax.sharding import PartitionSpec as P

HD = 128
SCALE = math.log2(math.e) / math.sqrt(HD)
FAR = 1e30
VMEM = 2 * 1024 * 1024


def rotated(block, axis, distance):
    size = lax.axis_size(axis)
    return lax.ppermute(block, axis, [(i, (i + distance) % size) for i in range(size)])


def shifted(block, axis, distance):
    size = lax.axis_size(axis)
    return lax.ppermute(block, axis, [(i, i + distance) for i in range(size - distance)])


def swapped(block, axis):
    size = lax.axis_size(axis)
    return lax.ppermute(block, axis, [(i, i ^ 1) for i in range(size)])


def scores(q, keys):
    return lax.dot_general(q, keys, (((1,), (1,)), ((), ())), preferred_element_type=jnp.float32)


def mix(weights, values):
    return jnp.dot(weights.astype(jnp.bfloat16), values, preferred_element_type=jnp.float32)


def columns(refs, first, cols, wide):
    return jnp.concatenate([r[:, cols if first + i else wide] for i, r in enumerate(refs)], axis=0)


def early_kernel(count, at, heads, *refs):
    q_refs, now, (mate_now, mate_back2, back2) = refs[:count], refs[count : 2 * count], refs[2 * count : 2 * count + 3]
    peak_ref, total_ref, mixed_ref = refs[2 * count + 3 :]
    frame = lax.axis_index("tm")
    odd = (frame % 2) == 1
    rows = q_refs[0].shape[0]

    for head in range(heads):
        cols = slice(head * HD, (head + 1) * HD)
        wide = slice((at + head) * HD, (at + head + 1) * HD)

        def pick(which):
            here = [r[which, :, cols if i else wide] for i, r in enumerate(now)]
            past = [jnp.where(odd, mate_now[which, :, wide], mate_back2[which, :, wide]), back2[which, :, wide]]
            return jnp.concatenate(here, axis=0), jnp.concatenate(past, axis=0)

        (k0, k1), (v0, v1) = pick(0), pick(1)
        for first in range(0, count, 2):
            some = q_refs[first : first + 2]
            span = slice(first * rows, (first + len(some)) * rows)
            q = columns(some, first, cols, wide)
            s0, s1 = scores(q, k0), scores(q, k1)
            s1 = jnp.concatenate(
                [jnp.where(frame >= 1, s1[:, :rows], -FAR), jnp.where(frame >= 2, s1[:, rows:], -FAR)], axis=1
            )
            peak = jnp.maximum(jnp.max(s0, axis=1, keepdims=True), jnp.max(s1, axis=1, keepdims=True))
            p0 = jnp.exp2((s0 - peak) * SCALE)
            p1 = jnp.exp2((s1 - peak) * SCALE)
            total = jnp.sum(p0, axis=1, keepdims=True) + jnp.sum(p1, axis=1, keepdims=True)
            peak_ref[span, cols] = jnp.broadcast_to(peak, (q.shape[0], HD))
            total_ref[span, cols] = jnp.broadcast_to(total, (q.shape[0], HD))
            mixed_ref[span, cols] = mix(p0, v0) + mix(p1, v1)


def late_kernel(count, at, heads, *refs):
    more = count - 1
    q_refs, (mate_now, mate_back2, back2) = refs[:count], (
        refs[count + i * more : count + (i + 1) * more] for i in range(3)
    )
    peak_ref, total_ref, mixed_ref = refs[count + 3 * more : count + 3 * more + 3]
    outs = refs[count + 3 * more + 3 :]
    frame = lax.axis_index("tm")
    odd = (frame % 2) == 1
    rows = q_refs[0].shape[0]

    for head in range(heads):
        cols = slice(head * HD, (head + 1) * HD)
        wide = slice((at + head) * HD, (at + head + 1) * HD)

        def pick(which):
            past = [jnp.where(odd, a[which, :, cols], b[which, :, cols]) for a, b in zip(mate_now, mate_back2)]
            return jnp.concatenate(past + [r[which, :, cols] for r in back2], axis=0)

        keys, vals = pick(0), pick(1)
        for first in range(0, count, 2):
            some = q_refs[first : first + 2]
            span = slice(first * rows, (first + len(some)) * rows)
            s = scores(columns(some, first, cols, wide), keys)
            s = jnp.concatenate(
                [jnp.where(frame >= 1, s[:, : more * rows], -FAR), jnp.where(frame >= 2, s[:, more * rows :], -FAR)],
                axis=1,
            )
            before = peak_ref[span, cols]
            peak = jnp.maximum(before, jnp.broadcast_to(jnp.max(s, axis=1, keepdims=True), before.shape))
            shrink = jnp.exp2((before - peak) * SCALE)
            p = jnp.exp2((s - jnp.concatenate([peak] * (2 * more * rows // HD), axis=1)) * SCALE)
            total = total_ref[span, cols] * shrink + jnp.sum(p, axis=1, keepdims=True)
            mixed = (mixed_ref[span, cols] * shrink + mix(p, vals)) * (1.0 / total)
            mixed = mixed.astype(jnp.bfloat16)
            for i in range(len(some)):
                outs[first + i][:, cols] = mixed[i * rows : (i + 1) * rows]


def call(kernel, arrays, shapes, work):
    return pl.pallas_call(
        kernel,
        out_shape=shapes,
        in_specs=[pl.BlockSpec(memory_space=pltpu.VMEM)] * len(arrays),
        out_specs=[pl.BlockSpec(memory_space=pltpu.VMEM)] * len(shapes),
        cost_estimate=pl.CostEstimate(flops=4 * work * HD, transcendentals=work, bytes_accessed=2**21),
        compiler_params=pltpu.CompilerParams(vmem_limit_bytes=VMEM * lax.axis_size("fsdp")),
    )(*arrays)


def early(at, queries, here, past):
    count = len(queries)
    rows, width = queries[1].shape
    work = width // HD * count * rows * (count + 2) * rows
    state = [jax.ShapeDtypeStruct((count * rows, width), jnp.float32)] * 3
    kernel = functools.partial(early_kernel, count, at, width // HD)
    return call(kernel, (*queries, *here, *past), state, work)


def late(at, queries, past, state):
    count = len(queries)
    rows, width = queries[1].shape
    work = width // HD * count * rows * 2 * (count - 1) * rows
    shapes = [jax.ShapeDtypeStruct((rows, width), jnp.bfloat16)] * count
    kernel = functools.partial(late_kernel, count, at, width // HD)
    return call(kernel, (*queries, *past, *state), shapes, work)


def cut_kernel(plan, count, *refs):
    arrays, outs, sems = refs[:count], refs[count:-1], refs[-1]
    size = lax.axis_size("fsdp")
    me = lax.axis_index("fsdp")
    copies = []
    for source, turn, start, width, out, slot in plan:
        owner = lax.rem(me + turn, size)
        heads = arrays[source].shape[2] // HD // size
        columns = pl.ds(pl.multiple_of((owner * heads + start) * HD, HD), width)
        target = outs[out] if slot is None else outs[out].at[slot]
        copies.append(pltpu.make_async_copy(arrays[source].at[0, :, columns], target, sems.at[len(copies)]))
    for copy in copies:
        copy.start()
    for copy in copies:
        copy.wait()


def cut(arrays, plan, shapes):
    return pl.pallas_call(
        functools.partial(cut_kernel, plan, len(arrays)),
        out_shape=[jax.ShapeDtypeStruct(x, jnp.bfloat16) for x in shapes],
        in_specs=[pl.BlockSpec(memory_space=pl.ANY)] * len(arrays),
        out_specs=[pl.BlockSpec(memory_space=pltpu.VMEM)] * len(shapes),
        scratch_shapes=[pltpu.SemaphoreType.DMA((len(plan),))],
        cost_estimate=pl.CostEstimate(flops=0, transcendentals=0, bytes_accessed=2**21),
        compiler_params=pltpu.CompilerParams(vmem_limit_bytes=VMEM * lax.axis_size("fsdp")),
    )(*arrays)


def join_kernel(places, *refs):
    blocks, out, sems = refs[:-2], refs[-2], refs[-1]
    size = lax.axis_size("fsdp")
    me = lax.axis_index("fsdp")
    heads = out.shape[2] // HD // size
    copies = []
    for block, (turn, start) in zip(blocks, places):
        owner = lax.rem(me + turn, size)
        columns = pl.ds(pl.multiple_of((owner * heads + start) * HD, HD), block.shape[1])
        copies.append(pltpu.make_async_copy(block, out.at[0, :, columns], sems.at[len(copies)]))
    for copy in copies:
        copy.start()
    for copy in copies:
        copy.wait()


def join(blocks, places, shape):
    return pl.pallas_call(
        functools.partial(join_kernel, places),
        out_shape=jax.ShapeDtypeStruct(shape, jnp.bfloat16),
        in_specs=[pl.BlockSpec(memory_space=pltpu.VMEM)] * len(blocks),
        out_specs=pl.BlockSpec(memory_space=pl.ANY),
        scratch_shapes=[pltpu.SemaphoreType.DMA((len(blocks),))],
        cost_estimate=pl.CostEstimate(flops=0, transcendentals=0, bytes_accessed=2**21),
        compiler_params=pltpu.CompilerParams(vmem_limit_bytes=VMEM * lax.axis_size("fsdp")),
        name="join",
    )(*blocks)


SHARES = (4, 4, 4)


def splits(heads):
    ends = [round(heads * sum(SHARES[: i + 1]) / sum(SHARES)) for i in range(len(SHARES))]
    sizes = [b - a for a, b in zip([0, *ends], ends)]
    return [n for n in sizes if n]


def body(queries, keys, values):
    size = lax.axis_size("fsdp")
    tokens, width = queries.shape[1], queries.shape[2] // size
    sizes = splits(width // HD)
    starts = [sum(sizes[:i]) for i in range(len(sizes))]
    groups = range(len(sizes))

    (own,) = cut((keys, values), ((0, 0, 0, width, 0, 0), (1, 0, 0, width, 0, 1)), [(2, tokens, width)])
    own_back2 = shifted(own, "tm", 2)
    plan, shapes = [(0, 0, 0, width, 0, None)], [(tokens, width)]
    for r in range(1, size):
        for g in groups:
            span = sizes[g] * HD
            plan += [(1, r, starts[g], span, len(shapes), 0), (2, r, starts[g], span, len(shapes), 1)]
            shapes.append((2, tokens, span))
            plan.append((0, r, starts[g], span, len(shapes), None))
            shapes.append((tokens, span))
    q_own, *sends = cut((queries, keys, values), tuple(plan), shapes)
    here, asked = [[own] for g in groups], [[q_own] for g in groups]
    for r in range(1, size):
        for g in groups:
            pair, query = sends[2 * ((r - 1) * len(sizes) + g) :][:2]
            here[g].append(rotated(pair, "fsdp", r))
            asked[g].append(rotated(query, "fsdp", r))
    mate_own = swapped(own, "tm")
    mate_own_back2 = swapped(own_back2, "tm")
    outs = []
    for g in groups:
        state = early(starts[g], asked[g], here[g], (mate_own, mate_own_back2, own_back2))
        back2 = [shifted(x, "tm", 2) for x in here[g][1:]]
        mate_now = [swapped(x, "tm") for x in here[g][1:]]
        mate_back2 = [swapped(x, "tm") for x in back2]
        outs.append(late(starts[g], asked[g], (*mate_now, *mate_back2, *back2), state))
    blocks, places = [], []
    for g in groups:
        for r in range(size):
            blocks.append(rotated(outs[g][r], "fsdp", -r) if r else outs[g][r])
            places.append((r, starts[g]))
    return join(blocks, places, queries.shape)


def solution(mesh):
    spec = P("tm", "fsdp", None)
    return jax.shard_map(body, mesh=mesh, in_specs=(spec, spec, spec), out_specs=spec, check_vma=False)
```

```python
import functools
import math

import jax
import jax.numpy as jnp
from jax import lax
from jax.experimental import pallas as pl
from jax.experimental.pallas import tpu as pltpu
from jax.sharding import PartitionSpec as P

HD = 128
SCALE = math.log2(math.e) / math.sqrt(HD)
FAR = 1e30
VMEM = 2 * 1024 * 1024


def rotated(block, axis, distance):
    size = lax.axis_size(axis)
    return lax.ppermute(block, axis, [(i, (i + distance) % size) for i in range(size)])


def shifted(block, axis, distance, parities=(0, 1)):
    size = lax.axis_size(axis)
    return lax.ppermute(block, axis, [(i, i + distance) for i in range(size - distance) if i % 2 in parities])


def swapped(block, axis):
    size = lax.axis_size(axis)
    return lax.ppermute(block, axis, [(i, i ^ 1) for i in range(size)])


def scores(q, keys):
    return lax.dot_general(q, keys, (((1,), (1,)), ((), ())), preferred_element_type=jnp.float32)


def mix(weights, values):
    return jnp.dot(weights.astype(jnp.bfloat16), values, preferred_element_type=jnp.float32)


def columns(refs, first, cols, wide):
    return jnp.concatenate([r[:, cols if first + i else wide] for i, r in enumerate(refs)], axis=0)


def chosen(odd, arrays, index):
    return arrays[0][index] if len(arrays) == 1 else jnp.where(odd, arrays[0][index], arrays[1][index])


def early_kernel(count, at, heads, *refs):
    q_refs, now, (mate_now, mate_back2) = refs[:count], refs[count : 2 * count], refs[2 * count : 2 * count + 2]
    back2 = refs[2 * count + 2 : -3]
    peak_ref, total_ref, mixed_ref = refs[-3:]
    frame = lax.axis_index("tm")
    odd = (frame % 2) == 1
    rows = q_refs[0].shape[0]

    for head in range(heads):
        cols = slice(head * HD, (head + 1) * HD)
        wide = slice((at + head) * HD, (at + head + 1) * HD)

        def pick(which):
            index = (which, slice(None), wide)
            here = [r[which, :, cols] if i else r[index] for i, r in enumerate(now)]
            past = [chosen(odd, (mate_now, mate_back2), index), chosen(odd, back2, index)]
            return jnp.concatenate(here, axis=0), jnp.concatenate(past, axis=0)

        (k0, k1), (v0, v1) = pick(0), pick(1)
        for first in range(0, count, 2):
            some = q_refs[first : first + 2]
            span = slice(first * rows, (first + len(some)) * rows)
            q = columns(some, first, cols, wide)
            s0, s1 = scores(q, k0), scores(q, k1)
            s1 = jnp.concatenate(
                [jnp.where(frame >= 1, s1[:, :rows], -FAR), jnp.where(frame >= 2, s1[:, rows:], -FAR)], axis=1
            )
            peak = jnp.maximum(jnp.max(s0, axis=1, keepdims=True), jnp.max(s1, axis=1, keepdims=True))
            p0 = jnp.exp2((s0 - peak) * SCALE)
            p1 = jnp.exp2((s1 - peak) * SCALE)
            total = jnp.sum(p0, axis=1, keepdims=True) + jnp.sum(p1, axis=1, keepdims=True)
            peak_ref[span, cols] = jnp.broadcast_to(peak, (q.shape[0], HD))
            total_ref[span, cols] = jnp.broadcast_to(total, (q.shape[0], HD))
            mixed_ref[span, cols] = mix(p0, v0) + mix(p1, v1)


def late_kernel(count, at, heads, kinds, *refs):
    more = count - 1
    q_refs = refs[:count]
    mate_now, mate_back2, *back2 = (refs[count + i * more : count + (i + 1) * more] for i in range(2 + kinds))
    peak_ref, total_ref, mixed_ref = refs[-3 - count : -count]
    outs = refs[-count:]
    frame = lax.axis_index("tm")
    odd = (frame % 2) == 1
    rows = q_refs[0].shape[0]

    for head in range(heads):
        cols = slice(head * HD, (head + 1) * HD)
        wide = slice((at + head) * HD, (at + head + 1) * HD)

        def pick(which):
            index = (which, slice(None), cols)
            past = [chosen(odd, x, index) for x in zip(mate_now, mate_back2)]
            return jnp.concatenate(past + [chosen(odd, x, index) for x in zip(*back2)], axis=0)

        keys, vals = pick(0), pick(1)
        for first in range(0, count, 2):
            some = q_refs[first : first + 2]
            span = slice(first * rows, (first + len(some)) * rows)
            s = scores(columns(some, first, cols, wide), keys)
            s = jnp.concatenate(
                [jnp.where(frame >= 1, s[:, : more * rows], -FAR), jnp.where(frame >= 2, s[:, more * rows :], -FAR)],
                axis=1,
            )
            before = peak_ref[span, cols]
            peak = jnp.maximum(before, jnp.broadcast_to(jnp.max(s, axis=1, keepdims=True), before.shape))
            shrink = jnp.exp2((before - peak) * SCALE)
            p = jnp.exp2((s - jnp.concatenate([peak] * (2 * more * rows // HD), axis=1)) * SCALE)
            total = total_ref[span, cols] * shrink + jnp.sum(p, axis=1, keepdims=True)
            mixed = (mixed_ref[span, cols] * shrink + mix(p, vals)) * (1.0 / total)
            mixed = mixed.astype(jnp.bfloat16)
            for i in range(len(some)):
                outs[first + i][:, cols] = mixed[i * rows : (i + 1) * rows]


def call(kernel, arrays, shapes, work):
    return pl.pallas_call(
        kernel,
        out_shape=shapes,
        in_specs=[pl.BlockSpec(memory_space=pltpu.VMEM)] * len(arrays),
        out_specs=[pl.BlockSpec(memory_space=pltpu.VMEM)] * len(shapes),
        cost_estimate=pl.CostEstimate(flops=4 * work * HD, transcendentals=work, bytes_accessed=2**21),
        compiler_params=pltpu.CompilerParams(vmem_limit_bytes=VMEM * lax.axis_size("fsdp")),
    )(*arrays)


def early(at, queries, here, past):
    count = len(queries)
    rows, width = queries[1].shape
    work = width // HD * count * rows * (count + 2) * rows
    state = [jax.ShapeDtypeStruct((count * rows, width), jnp.float32)] * 3
    kernel = functools.partial(early_kernel, count, at, width // HD)
    return call(kernel, (*queries, *here, *past), state, work)


def late(at, queries, mates, back2, state):
    count = len(queries)
    rows, width = queries[1].shape
    work = width // HD * count * rows * 2 * (count - 1) * rows
    shapes = [jax.ShapeDtypeStruct((rows, width), jnp.bfloat16)] * count
    kernel = functools.partial(late_kernel, count, at, width // HD, len(back2))
    return call(kernel, (*queries, *mates, *sum(back2, []), *state), shapes, work)


def cut_kernel(plan, count, *refs):
    arrays, outs, sems = refs[:count], refs[count:-1], refs[-1]
    size = lax.axis_size("fsdp")
    me = lax.axis_index("fsdp")
    copies = []
    for source, turn, start, width, out, slot in plan:
        owner = lax.rem(me + turn, size)
        heads = arrays[source].shape[2] // HD // size
        columns = pl.ds(pl.multiple_of((owner * heads + start) * HD, HD), width)
        target = outs[out] if slot is None else outs[out].at[slot]
        copies.append(pltpu.make_async_copy(arrays[source].at[0, :, columns], target, sems.at[len(copies)]))
    for copy in copies:
        copy.start()
    for copy in copies:
        copy.wait()


def cut(arrays, plan, shapes):
    return pl.pallas_call(
        functools.partial(cut_kernel, plan, len(arrays)),
        out_shape=[jax.ShapeDtypeStruct(x, jnp.bfloat16) for x in shapes],
        in_specs=[pl.BlockSpec(memory_space=pltpu.HBM)] * len(arrays),
        out_specs=[pl.BlockSpec(memory_space=pltpu.VMEM)] * len(shapes),
        scratch_shapes=[pltpu.SemaphoreType.DMA((len(plan),))],
        cost_estimate=pl.CostEstimate(flops=0, transcendentals=0, bytes_accessed=2**21),
        compiler_params=pltpu.CompilerParams(vmem_limit_bytes=VMEM * lax.axis_size("fsdp")),
    )(*arrays)


def join_kernel(places, filled, *refs):
    blocks, out, sems = refs[filled:-2], refs[-2], refs[-1]
    size = lax.axis_size("fsdp")
    me = lax.axis_index("fsdp")
    heads = out.shape[2] // HD // size
    copies = []
    for block, (turn, start) in zip(blocks, places):
        owner = lax.rem(me + turn, size)
        columns = pl.ds(pl.multiple_of((owner * heads + start) * HD, HD), block.shape[1])
        copies.append(pltpu.make_async_copy(block, out.at[0, :, columns], sems.at[len(copies)]))
    for copy in copies:
        copy.start()
    for copy in copies:
        copy.wait()


def join(blocks, places, shape, result=()):
    return pl.pallas_call(
        functools.partial(join_kernel, places, len(result)),
        out_shape=jax.ShapeDtypeStruct(shape, jnp.bfloat16),
        in_specs=[pl.BlockSpec(memory_space=pltpu.HBM)] * len(result)
        + [pl.BlockSpec(memory_space=pltpu.VMEM)] * len(blocks),
        out_specs=pl.BlockSpec(memory_space=pltpu.HBM),
        scratch_shapes=[pltpu.SemaphoreType.DMA((len(blocks),))],
        input_output_aliases={0: 0} if result else {},
        cost_estimate=pl.CostEstimate(flops=0, transcendentals=0, bytes_accessed=2**18),
        compiler_params=pltpu.CompilerParams(vmem_limit_bytes=VMEM * lax.axis_size("fsdp")),
        name="join",
    )(*result, *blocks)


SHARES = (6, 3, 3)
BOTH = ((0, 1),)
FIRST, LAST = BOTH, BOTH


def splits(heads):
    ends = [round(heads * sum(SHARES[: i + 1]) / sum(SHARES)) for i in range(len(SHARES))]
    sizes = [b - a for a, b in zip([0, *ends], ends)]
    return [n for n in sizes if n]


def body(queries, keys, values):
    size = lax.axis_size("fsdp")
    tokens, width = queries.shape[1], queries.shape[2] // size
    sizes = splits(width // HD)
    starts = [sum(sizes[:i]) for i in range(len(sizes))]
    groups = range(len(sizes))

    at = lax.axis_index("fsdp") * width
    own = jnp.stack([lax.dynamic_slice_in_dim(x[0], at, width, 1) for x in (keys, values)])
    own, queries, keys, values = lax.optimization_barrier((own, queries, keys, values))
    plan, shapes = [(0, 0, 0, width, 0, None)], [(tokens, width)]
    for r in range(1, size):
        for g in groups:
            span = sizes[g] * HD
            plan += [(1, r, starts[g], span, len(shapes), 0), (2, r, starts[g], span, len(shapes), 1)]
            shapes.append((2, tokens, span))
            plan.append((0, r, starts[g], span, len(shapes), None))
            shapes.append((tokens, span))
    q_own, *sends = cut((queries, keys, values), tuple(plan), shapes)

    def moved(block, parities):
        result = []
        for parity in parities:
            result.append(shifted(block, "tm", 2, parity))
        return result

    back2 = moved(own, FIRST)
    past = [swapped(own, "tm")]
    past += [swapped(back2[0], "tm"), *back2]
    here, asked = [[] for g in groups], [[q_own] for g in groups]
    for r in range(1, size):
        for g in groups:
            pair, query = sends[2 * ((r - 1) * len(sizes) + g) :][:2]
            here[g].append(rotated(pair, "fsdp", r))
            asked[g].append(rotated(query, "fsdp", r))
    outs = []
    for g in groups:
        state = early(starts[g], asked[g], [own, *here[g]], past)
        back2 = [moved(x, LAST if g == groups[-1] else BOTH) for x in here[g]]
        mate_now = [swapped(x, "tm") for x in here[g]]
        mate_back2 = [swapped(x[0], "tm") for x in back2]
        outs.append(late(starts[g], asked[g], mate_now + mate_back2, [list(x) for x in zip(*back2)], state))
    blocks = {(r, g): outs[g][r] for g in groups for r in range(size)}
    for g in groups:
        for r in range(1, size):
            blocks[r, g] = rotated(blocks[r, g], "fsdp", -r)
    tail = [(r, groups[-1]) for r in range(1, size)]
    result = ()
    for part in ([x for x in blocks if x not in tail], tail):
        result = (join([blocks[x] for x in part], tuple((r, starts[g]) for r, g in part), queries.shape, result),)
    return result[0]


def solution(mesh):
    spec = P("tm", "fsdp", None)
    return jax.shard_map(body, mesh=mesh, in_specs=(spec, spec, spec), out_specs=spec, check_vma=False)
```
